128 devices in a mesh: ta: 16 (over y, x_lo, core), ba: 8 (over z, x_hi).
Axes of the slice: x: 4 (x_hi: 2, x_lo: 2; x = x_hi * 2 + x_lo), y: 4, z: 4, core: 2. Of those that a mesh axis runs over, the one named last changes fastest.
Arguments:
- search_block: float32 [16, 2, 4, 3, 32, 512], P(None, None, None, None, 'ta'), may hold values from -140 to 140
- kept_basis: float32 [128, 2, 4, 3, 32, 512], P('ba', None, None, None, 'ta'), may hold values from -4 to 4
- gauge_links: float32 [4, 2, 3, 3, 32, 512], P(None, None, None, None, 'ta'), may hold values from -1 to 1, as said below
- clover_term: float32 [2, 2, 6, 6, 32, 512], P(None, None, None, None, 'ta'), may hold values from -0.5 to 1.3, as said below
Outputs:
- ortho_block: float32 [16, 2, 4, 3, 32, 512], P('ba', None, None, None, 'ta')
- correlations: float32 [2, 128, 16], P(None, 'ba')
The draws below stay inside these ranges and needn't reach their ends.
Inputs may be any that keep to these rules, and one draw needn't show every extreme that they name: `gauge_links`: every link matrix is special unitary. `clover_term`: each 6x6 block of the clover term is Hermitian.
All inputs are finite; a program needn't handle non-finite values.
Results may differ from the reference program's by a relative error of at most 0.0002.
Values sent between devices are 32-bit elements; how exact they have to be, the bound alone decides.
A program may use at most 128 MiB of HBM per device.

```python
import math
import jax
import jax.numpy as jnp
import numpy as np
from jax import lax

BLOCK = 16
KEPT = 128
LS = 8
NT = 32


def basis_values(key):
    base_key = jax.random.fold_in(key, 101)
    draw_shape = (KEPT, 2, 4, 3, NT, LS ** 3)
    return jax.random.truncated_normal(base_key, -4.0, 4.0, draw_shape, jnp.float32)


def draw_kept_basis(key, part):
    return basis_values(key)


def draw_search_block(key, part):
    kept_values = basis_values(key)
    chosen = jax.random.permutation(jax.random.fold_in(key, 202), KEPT)[:BLOCK]
    site_count = LS ** 3
    noise = jax.random.truncated_normal(jax.random.fold_in(key, 203), -4.0, 4.0, (BLOCK, 2, 4, 3, NT, site_count), jnp.float32)
    time_index = jnp.arange(NT, dtype=jnp.float32)
    ramp = jnp.exp(math.log(3.0) * time_index / max(NT - 1, 1)) / math.sqrt(3.0)
    spread = math.log(4.0)
    mixed = 0.8 * kept_values[chosen] + 0.6 * noise
    row_scale = jnp.exp(spread * (jax.random.uniform(jax.random.fold_in(key, 205), (1, 1, 1, 1, NT, site_count), jnp.float32) - 0.5))
    column_scale = jnp.exp(spread * (jax.random.uniform(jax.random.fold_in(key, 206), (BLOCK, 1, 1, 1, 1, 1), jnp.float32) - 0.5))
    return mixed * row_scale * column_scale * ramp[:, None]


def embedded(key, first, second):
    draw_shape = (4, NT, LS ** 3)
    angle_theta = jax.random.uniform(jax.random.fold_in(key, 1), draw_shape, jnp.float32, 0.0, 2.0 * math.pi)
    angle_alpha = jax.random.uniform(jax.random.fold_in(key, 2), draw_shape, jnp.float32, 0.0, 2.0 * math.pi)
    angle_beta = jax.random.uniform(jax.random.fold_in(key, 3), draw_shape, jnp.float32, 0.0, 2.0 * math.pi)
    diag_re = jnp.cos(angle_theta) * jnp.cos(angle_alpha)
    diag_im = jnp.cos(angle_theta) * jnp.sin(angle_alpha)
    off_re = jnp.sin(angle_theta) * jnp.cos(angle_beta)
    off_im = jnp.sin(angle_theta) * jnp.sin(angle_beta)
    identity = jnp.broadcast_to(jnp.eye(3, dtype=jnp.float32)[:, :, None, None, None], (3, 3) + draw_shape)
    mat_re = identity.at[first, first].set(diag_re).at[first, second].set(off_re).at[second, first].set(-off_re).at[second, second].set(diag_re)
    mat_im = jnp.zeros_like(identity).at[first, first].set(diag_im).at[first, second].set(off_im).at[second, first].set(off_im).at[second, second].set(-diag_im)
    return (mat_re, mat_im)


def matrix_product(left_re, left_im, right_re, right_im):
    out_re = jnp.sum(left_re[:, :, None] * right_re[None] - left_im[:, :, None] * right_im[None], axis=1)
    out_im = jnp.sum(left_re[:, :, None] * right_im[None] + left_im[:, :, None] * right_re[None], axis=1)
    return (out_re, out_im)


def draw_gauge_links(key, part):
    first_re, first_im = embedded(jax.random.fold_in(key, 11), 0, 1)
    second_re, second_im = embedded(jax.random.fold_in(key, 12), 1, 2)
    third_re, third_im = embedded(jax.random.fold_in(key, 13), 0, 2)
    step_re, step_im = matrix_product(first_re, first_im, second_re, second_im)
    final_re, final_im = matrix_product(step_re, step_im, third_re, third_im)
    stacked = jnp.stack([final_re, final_im], 0)
    return jnp.transpose(stacked, (3, 0, 1, 2, 4, 5))


def draw_clover_term(key, part):
    site_count = LS ** 3
    draw_shape = (2, 6, 6, NT, site_count)
    raw_re = 0.15 * jax.random.truncated_normal(jax.random.fold_in(key, 31), -2.0, 2.0, draw_shape, jnp.float32)
    raw_im = 0.15 * jax.random.truncated_normal(jax.random.fold_in(key, 32), -2.0, 2.0, draw_shape, jnp.float32)
    symmetric_re = 0.5 * (raw_re + raw_re.swapaxes(1, 2))
    antisym_im = 0.5 * (raw_im - raw_im.swapaxes(1, 2))
    diagonal = jax.random.uniform(jax.random.fold_in(key, 33), (2, 6, NT, site_count), jnp.float32, 0.7, 1.3)
    eye_six = jnp.eye(6, dtype=jnp.float32)[None, :, :, None, None]
    hermit_re = symmetric_re * (1.0 - eye_six) + eye_six * diagonal[:, :, None]
    return jnp.stack([hermit_re, antisym_im], 1)


def setup_inputs(seed: int = 0) -> dict:
    arg_keys = jax.random.split(jax.random.key(seed), 5)
    search_block = draw_search_block(jax.random.fold_in(arg_keys[4], 71), 0)
    kept_basis = draw_kept_basis(jax.random.fold_in(arg_keys[4], 71), 0)
    gauge_links = draw_gauge_links(jax.random.fold_in(arg_keys[4], 71), 0)
    clover_term = draw_clover_term(jax.random.fold_in(arg_keys[4], 71), 0)
    return dict(search_block=search_block, kept_basis=kept_basis, gauge_links=gauge_links, clover_term=clover_term)


HOPPING = 0.13
HIGHEST = lax.Precision.HIGHEST

def gamma_tables():
    gamma_re = np.zeros((4, 4, 4), np.float32)
    gamma_im = np.zeros((4, 4, 4), np.float32)
    gamma_im[0, 0:2, 2:4] = [[0, -1], [-1, 0]]
    gamma_im[0, 2:4, 0:2] = [[0, 1], [1, 0]]
    gamma_re[1, 0:2, 2:4] = [[0, -1], [1, 0]]
    gamma_re[1, 2:4, 0:2] = [[0, 1], [-1, 0]]
    gamma_im[2, 0:2, 2:4] = [[-1, 0], [0, 1]]
    gamma_im[2, 2:4, 0:2] = [[1, 0], [0, -1]]
    gamma_re[3, 0:2, 2:4] = np.eye(2)
    gamma_re[3, 2:4, 0:2] = np.eye(2)
    return (gamma_re, gamma_im)

def gamma_apply(direction, spinor):
    tables_re, tables_im = gamma_tables()
    field_re = spinor[:, 0]
    field_im = spinor[:, 1]
    out_re = jnp.zeros_like(field_re)
    out_im = jnp.zeros_like(field_im)
    if np.any(tables_re[direction]):
        matrix = jnp.asarray(tables_re[direction])
        out_re = out_re + jnp.einsum('as,vsctx->vactx', matrix, field_re, precision=HIGHEST)
        out_im = out_im + jnp.einsum('as,vsctx->vactx', matrix, field_im, precision=HIGHEST)
    if np.any(tables_im[direction]):
        matrix = jnp.asarray(tables_im[direction])
        out_re = out_re - jnp.einsum('as,vsctx->vactx', matrix, field_im, precision=HIGHEST)
        out_im = out_im + jnp.einsum('as,vsctx->vactx', matrix, field_re, precision=HIGHEST)
    return jnp.stack([out_re, out_im], 1)

def gamma_five(spinor):
    return jnp.concatenate([spinor[:, :, :2], -spinor[:, :, 2:]], axis=2)

def colour(link_dir, spinor):
    link_re = link_dir[0][None, None]
    link_im = link_dir[1][None, None]
    field_re = spinor[:, 0][:, :, None]
    field_im = spinor[:, 1][:, :, None]
    out_re = lax.optimization_barrier(jnp.sum(link_re * field_re - link_im * field_im, axis=3))
    out_im = lax.optimization_barrier(jnp.sum(link_re * field_im + link_im * field_re, axis=3))
    return jnp.stack([out_re, out_im], 1)

def dagger(link_dir):
    return jnp.stack([link_dir[0].swapaxes(0, 1), -link_dir[1].swapaxes(0, 1)], 0)

def shift_space(values, stride, forward):
    coordinate = jnp.arange(values.shape[-1]) // stride % LS
    if forward:
        return jnp.where(coordinate == LS - 1, jnp.roll(values, (LS - 1) * stride, axis=-1), jnp.roll(values, -stride, axis=-1))
    return jnp.where(coordinate == 0, jnp.roll(values, -(LS - 1) * stride, axis=-1), jnp.roll(values, stride, axis=-1))

def space_hops(spinor, link_field):
    hop_total = jnp.zeros_like(spinor)
    strides = (LS * LS, LS, 1)
    for direction in range(3):
        stride = strides[direction]
        link_dir = link_field[direction]
        ahead_term = colour(link_dir, shift_space(spinor, stride, True))
        behind = colour(dagger(shift_space(link_dir, stride, False)), shift_space(spinor, stride, False))
        hop_total = hop_total + (ahead_term + behind) - gamma_apply(direction, ahead_term - behind)
    return hop_total

def clover_apply(clover, spinor):
    vectors = spinor.shape[0]
    pieces = []
    for chiral in range(2):
        chiral_part = spinor[:, :, 2 * chiral:2 * chiral + 2]
        flat_part = chiral_part.reshape(vectors, 2, 6, chiral_part.shape[-2], chiral_part.shape[-1])
        mat_re = clover[chiral, 0][None]
        mat_im = clover[chiral, 1][None]
        vec_re = flat_part[:, 0][:, None]
        vec_im = flat_part[:, 1][:, None]
        out_re = lax.optimization_barrier(jnp.sum(mat_re * vec_re - mat_im * vec_im, axis=2))
        out_im = lax.optimization_barrier(jnp.sum(mat_re * vec_im + mat_im * vec_re, axis=2))
        pieces.append(jnp.stack([out_re, out_im], 1).reshape(chiral_part.shape))
    return jnp.concatenate(pieces, axis=2)

def dirac_apply(spinor, link_field, clover):
    slices = spinor.shape[4]
    time_index = jnp.arange(slices)
    sign_ahead = jnp.where(time_index == slices - 1, -1.0, 1.0).astype(spinor.dtype)
    sign_behind = jnp.where(time_index == 0, -1.0, 1.0).astype(spinor.dtype)
    ahead_field = jnp.roll(spinor, -1, axis=4) * sign_ahead[:, None]
    behind_field = jnp.roll(spinor, 1, axis=4) * sign_behind[:, None]
    link_time = link_field[3]
    ahead_term = colour(link_time, ahead_field)
    behind = colour(dagger(jnp.roll(link_time, 1, axis=3)), behind_field)
    hops = space_hops(spinor, link_field) + (ahead_term + behind) - gamma_apply(3, ahead_term - behind)
    return clover_apply(clover, spinor) - HOPPING * hops

def inner_product(left_re, left_im, right_re, right_im, norm_scale):
    real_part = jnp.einsum('kcn,jcn->kj', left_re, right_re, precision=HIGHEST) + jnp.einsum('kcn,jcn->kj', left_im, right_im, precision=HIGHEST)
    imag_part = jnp.einsum('kcn,jcn->kj', left_re, right_im, precision=HIGHEST) - jnp.einsum('kcn,jcn->kj', left_im, right_re, precision=HIGHEST)
    return (real_part * norm_scale, imag_part * norm_scale)

def combine_basis(coef_re, coef_im, vec_re, vec_im):
    out_re = jnp.einsum('kj,kcn->jcn', coef_re, vec_re, precision=HIGHEST) - jnp.einsum('kj,kcn->jcn', coef_im, vec_im, precision=HIGHEST)
    out_im = jnp.einsum('kj,kcn->jcn', coef_im, vec_re, precision=HIGHEST) + jnp.einsum('kj,kcn->jcn', coef_re, vec_im, precision=HIGHEST)
    return (out_re, out_im)

def cholesky_complex(gram_re, gram_im):
    matrix_order = gram_re.shape[0]
    lower_re = jnp.zeros_like(gram_re)
    lower_im = jnp.zeros_like(gram_im)
    index_row = jnp.arange(matrix_order)
    for column in range(matrix_order):
        row_re = lower_re[column]
        row_im = lower_im[column]
        acc_re = gram_re[:, column] - lax.optimization_barrier(jnp.sum(lower_re * row_re[None, :] + lower_im * row_im[None, :], axis=1))
        acc_im = gram_im[:, column] - lax.optimization_barrier(jnp.sum(lower_im * row_re[None, :] - lower_re * row_im[None, :], axis=1))
        pivot_value = jnp.sqrt(acc_re[column])
        below_mask = index_row > column
        new_re = jnp.where(index_row == column, pivot_value, jnp.where(below_mask, acc_re / pivot_value, 0.0))
        new_im = jnp.where(below_mask, acc_im / pivot_value, 0.0)
        lower_re = lower_re.at[:, column].set(new_re)
        lower_im = lower_im.at[:, column].set(new_im)
    return (lower_re, lower_im)

def invert_lower(lower_re, lower_im):
    matrix_order = lower_re.shape[0]
    inverse_re = jnp.zeros_like(lower_re)
    inverse_im = jnp.zeros_like(lower_im)
    index_row = jnp.arange(matrix_order)
    for row_index in range(matrix_order):
        row_re = lower_re[row_index]
        row_im = lower_im[row_index]
        sum_re = lax.optimization_barrier(jnp.sum(row_re[:, None] * inverse_re - row_im[:, None] * inverse_im, axis=0))
        sum_im = lax.optimization_barrier(jnp.sum(row_re[:, None] * inverse_im + row_im[:, None] * inverse_re, axis=0))
        unit_row = jnp.where(index_row == row_index, 1.0, 0.0).astype(lower_re.dtype)
        pivot_value = lower_re[row_index, row_index]
        inverse_re = inverse_re.at[row_index].set((unit_row - sum_re) / pivot_value)
        inverse_im = inverse_im.at[row_index].set(-sum_im / pivot_value)
    return (inverse_re, inverse_im)

def reference(search_block, kept_basis, gauge_links, clover_term):
    first_apply = dirac_apply(search_block, gauge_links, clover_term)
    applied = gamma_five(dirac_apply(gamma_five(first_apply), gauge_links, clover_term))
    block_size = search_block.shape[0]
    kept_size = kept_basis.shape[0]
    site_count = search_block.shape[4] * search_block.shape[5]
    norm_scale = 1.0 / (24.0 * site_count)
    applied_re = applied[:, 0].reshape(block_size, 12, site_count)
    applied_im = applied[:, 1].reshape(block_size, 12, site_count)
    basis_re = kept_basis[:, 0].reshape(kept_size, 12, site_count)
    basis_im = kept_basis[:, 1].reshape(kept_size, 12, site_count)
    over_re, over_im = inner_product(basis_re, basis_im, applied_re, applied_im, norm_scale)
    proj_re, proj_im = combine_basis(over_re, over_im, basis_re, basis_im)
    rest_re = applied_re - proj_re
    rest_im = applied_im - proj_im
    gram_re, gram_im = inner_product(rest_re, rest_im, rest_re, rest_im, norm_scale)
    lower_re, lower_im = cholesky_complex(gram_re, gram_im)
    inverse_re, inverse_im = invert_lower(lower_re, lower_im)
    ortho_re, ortho_im = combine_basis(inverse_re.T, -inverse_im.T, rest_re, rest_im)
    ortho_out = jnp.stack([ortho_re, ortho_im], 1).reshape(search_block.shape)
    return (ortho_out, jnp.stack([over_re, over_im], 0))
```

```python
import jax
import jax.numpy as jnp
from jax import lax
from jax.experimental import pallas as pl
from jax.experimental.pallas import tpu as pltpu
from jax.sharding import PartitionSpec as P

MESH = pl.DeviceIdType.MESH
F32 = jnp.float32
BF16 = jnp.bfloat16

HOPPING = 0.13
NTA, NBA = 16, 8
BLOCK = 16
KEPT = 128
GROUP = KEPT // NBA
MINE = BLOCK // NBA
COMPS = 24
PLANES = 12
LANES = 128
WIDE = PLANES * LANES

ISIGMA = (
    ((1, True, 1), (0, True, 1)),
    ((1, False, 1), (0, False, -1)),
    ((0, True, 1), (1, True, -1)),
)

NT_DIMS = (((1,), (1,)), ((), ()))
NN_DIMS = (((1,), (0,)), ((), ()))


def split(value):
    high = value.astype(BF16)
    return high, (value - high.astype(F32)).astype(BF16)


def matmul(left, right, dims):
    return lax.dot_general(left, right, dims, preferred_element_type=F32)


def comp(ri, spin, colour):
    return ri * 12 + spin * 3 + colour


def half(ri, spin, colour):
    return ri * 6 + spin * 3 + colour


def add_phase(base, other, imag, sign):
    if imag:
        other = (other[1], other[0])
        signs = (-sign, sign)
    else:
        signs = (sign, sign)
    return tuple(b + o if s > 0 else b - o for b, o, s in zip(base, other, signs))


def kernel(
    search, basis, links, clover, out, corr,
    psi, lk, cl, acc, h_t, b_t, dn, up, rdn, rup,
    basis_all, b_hi, b_lo, a_all, xf, x_hi, x_lo, cm, c_part, c_ba, c_sum, c_ta, c_full,
    wm, r_hi, r_lo, g_part, g_ta, g_sum, g_ba, vm, osend,
    in_sem, hs, hr, bs, br, as_, ar, cs1, cr1, cs2, cr2, gs1, gr1, gs2, gr2, os_, or_,
):
    ta = lax.axis_index("ta")
    ba = lax.axis_index("ba")
    above = (lax.rem(ta + 1, NTA), ba)
    below = (lax.rem(ta + NTA - 1, NTA), ba)

    def ta_peer(k):
        return lax.rem(ta + k, NTA)

    def ba_peer(k):
        return lax.rem(ba + k, NBA)

    barrier = pltpu.get_barrier_semaphore()
    for k in range(1, NTA):
        pl.semaphore_signal(barrier, inc=1, device_id=(ta_peer(k), ba), device_id_type=MESH)
    for k in range(1, NBA):
        pl.semaphore_signal(barrier, inc=1, device_id=(ta, ba_peer(k)), device_id_type=MESH)

    own = pl.multiple_of(ba * MINE * COMPS, 8)
    load_psi = pltpu.make_async_copy(
        search.at[pl.ds(own, MINE * COMPS)], psi.at[0], in_sem.at[0]
    )
    load_links = pltpu.make_async_copy(links, lk, in_sem.at[1])
    load_clover = pltpu.make_async_copy(clover, cl, in_sem.at[2])
    load_basis = pltpu.make_async_copy(basis.at[:, ba], basis_all.at[pl.ds(pl.multiple_of(ba * GROUP * COMPS, 8), GROUP * COMPS)], br.at[ba])
    load_psi.start()
    load_links.start()
    load_clover.start()
    load_basis.start()

    lane = lax.broadcasted_iota(jnp.int32, (8, LANES), 1)
    sub = lax.broadcasted_iota(jnp.int32, (8, LANES), 0)
    z_lane = lane % 8
    y_lane = (lane // 8) % 8
    z_last, z_first = z_lane == 7, z_lane == 0
    y_last, y_first = y_lane == 7, y_lane == 0
    x_even = lane < 64
    t_odd = sub % 2 == 1
    sign_last = jnp.where(ta == NTA - 1, -1.0, 1.0).astype(F32)
    sign_first = jnp.where(ta == 0, -1.0, 1.0).astype(F32)

    def lroll(value, shift):
        return pltpu.roll(value, shift, 1)

    def sroll(value, shift):
        return pltpu.roll(value, shift, 0)

    def ahead(value, mu):
        if mu == 0:
            turned = lroll(value, 64)
            return jnp.where(x_even, turned, sroll(turned, 6))
        if mu == 1:
            return jnp.where(y_last, lroll(value, 56), lroll(value, 120))
        return jnp.where(z_last, lroll(value, 7), lroll(value, 127))

    def behind(value, mu):
        if mu == 0:
            turned = lroll(value, 64)
            return jnp.where(x_even, sroll(turned, 2), turned)
        if mu == 1:
            return jnp.where(y_first, lroll(value, 72), lroll(value, 8))
        return jnp.where(z_first, lroll(value, 121), lroll(value, 1))

    def link(mu, row, col):
        place = mu * 18 + row * 3 + col
        return lk[place], lk[place + 9]

    def times_link(mu, vec):
        result = []
        for row in range(3):
            re = im = None
            for col in range(3):
                ur, ui = link(mu, row, col)
                vr, vi = vec[col]
                tr, ti = ur * vr - ui * vi, ur * vi + ui * vr
                re, im = (tr, ti) if re is None else (re + tr, im + ti)
            result.append((re, im))
        return result

    def times_dagger(mu, vec):
        result = []
        for row in range(3):
            re = im = None
            for col in range(3):
                ur, ui = link(mu, col, row)
                vr, vi = vec[col]
                tr, ti = ur * vr + ui * vi, ur * vi - ui * vr
                re, im = (tr, ti) if re is None else (re + tr, im + ti)
            result.append((re, im))
        return result

    def time_prepare(a):
        def one(v, carry):
            def field(spin, colour):
                base = v * COMPS
                return psi[a, base + comp(0, spin, colour)], psi[a, base + comp(1, spin, colour)]

            for spin in range(2):
                sums = []
                for colour in range(3):
                    upper, lower = field(spin, colour), field(spin + 2, colour)
                    for ri in range(2):
                        h_t[v * 12 + half(ri, spin, colour)] = upper[ri] - lower[ri]
                    sums.append((upper[0] + lower[0], upper[1] + lower[1]))
                linked = times_dagger(3, sums)
                for colour in range(3):
                    for ri in range(2):
                        b_t[v * 12 + half(ri, spin, colour)] = linked[colour][ri]
            return carry

        lax.fori_loop(0, MINE, one, 0)
        for i in range(12):
            dn[a, i] = jnp.where(t_odd, sroll(h_t[12 + i], 1), h_t[i])
            up[a, i] = jnp.where(t_odd, b_t[12 + i], sroll(b_t[i], 7))

    def halo_copies(a):
        down = pltpu.make_async_remote_copy(
            src_ref=dn.at[a], dst_ref=rdn.at[a], send_sem=hs.at[a, 0], recv_sem=hr.at[a, 0],
            device_id=below, device_id_type=MESH,
        )
        upward = pltpu.make_async_remote_copy(
            src_ref=up.at[a], dst_ref=rup.at[a], send_sem=hs.at[a, 1], recv_sem=hr.at[a, 1],
            device_id=above, device_id_type=MESH,
        )
        return down, upward

    def local_part(a):
        def one(v, carry):
            base = v * COMPS

            def field(spin, colour):
                return psi[a, base + comp(0, spin, colour)], psi[a, base + comp(1, spin, colour)]

            for chiral in range(2):
                vec = [field(2 * chiral + i // 3, i % 3) for i in range(6)]
                for row in range(6):
                    re = im = None
                    for col in range(6):
                        place = chiral * 72 + row * 6 + col
                        cr, ci = cl[place], cl[place + 36]
                        vr, vi = vec[col]
                        tr, ti = cr * vr - ci * vi, cr * vi + ci * vr
                        re, im = (tr, ti) if re is None else (re + tr, im + ti)
                    spin = 2 * chiral + row // 3
                    acc[base + comp(0, spin, row % 3)] = re
                    acc[base + comp(1, spin, row % 3)] = im
            for mu in range(3):
                for spin in range(2):
                    source, imag, sign = ISIGMA[mu][spin]
                    forward, backward = [], []
                    for colour in range(3):
                        upper, lower = field(spin, colour), field(2 + source, colour)
                        minus = add_phase(upper, lower, imag, sign)
                        plus = add_phase(upper, lower, imag, -sign)
                        forward.append(tuple(ahead(value, mu) for value in minus))
                        backward.append(plus)
                    forward = times_link(mu, forward)
                    backward = times_dagger(mu, backward)
                    backward = [tuple(behind(value, mu) for value in pair) for pair in backward]
                    target = [s for s in range(2) if ISIGMA[mu][s][0] == spin][0]
                    _, imag, sign = ISIGMA[mu][target]
                    for colour in range(3):
                        f, b = forward[colour], backward[colour]
                        for ri in range(2):
                            place = base + comp(ri, spin, colour)
                            acc[place] = acc[place] + (f[ri] + b[ri])
                        places = [base + comp(ri, 2 + target, colour) for ri in range(2)]
                        total = add_phase(
                            (acc[places[0]], acc[places[1]]), (b[0] - f[0], b[1] - f[1]), imag, sign
                        )
                        acc[places[0]] = total[0]
                        acc[places[1]] = total[1]
            return carry

        lax.fori_loop(0, MINE, one, 0)

    def time_finish(a):
        for v in range(MINE):
            for spin in range(2):
                front, back = [], []
                for colour in range(3):
                    f, b = [], []
                    for ri in range(2):
                        i = half(ri, spin, colour)
                        got, low = rdn[a, i] * sign_last, rup[a, i] * sign_first
                        got = sroll(got, 1) if v == 0 else got
                        low = low if v == 0 else sroll(low, 7)
                        f.append(jnp.where(t_odd, got, sroll(h_t[v * 12 + i], 7)))
                        b.append(jnp.where(t_odd, sroll(b_t[v * 12 + i], 1), low))
                    front.append(tuple(f))
                    back.append(tuple(b))
                front = times_link(3, front)
                for colour in range(3):
                    for ri in range(2):
                        f, b = front[colour][ri], back[colour][ri]
                        upper = v * COMPS + comp(ri, spin, colour)
                        lower = v * COMPS + comp(ri, spin + 2, colour)
                        psi[a + 1, upper] = acc[upper] + (f + b)
                        psi[a + 1, lower] = (f - b) - acc[lower]

    load_psi.wait()
    load_links.wait()

    def scale_link(i, carry):
        lk[i] = lk[i] * (-HOPPING)
        return carry

    lax.fori_loop(0, 72, scale_link, 0)
    time_prepare(0)
    load_clover.wait()

    pl.semaphore_wait(barrier, NTA + NBA - 2)

    first_halo = halo_copies(0)
    for copy in first_halo:
        copy.start()

    def block_of(ref, place, size):
        return ref.at[pl.ds(pl.multiple_of(place * size, 8), size)]

    basis_sends = [
        pltpu.make_async_remote_copy(
            src_ref=basis.at[:, ba_peer(k)], dst_ref=block_of(basis_all, ba, GROUP * COMPS),
            send_sem=bs.at[k], recv_sem=br.at[ba],
            device_id=(ta, ba_peer(k)), device_id_type=MESH,
        )
        for k in range(1, NBA)
    ]
    for copy in basis_sends:
        copy.start()

    local_part(0)
    for copy in first_halo:
        copy.wait_recv()
    time_finish(0)
    time_prepare(1)
    second_halo = halo_copies(1)
    for copy in second_halo:
        copy.start()
    local_part(1)
    for copy in second_halo:
        copy.wait_recv()
    time_finish(1)

    applied_sends = [
        pltpu.make_async_remote_copy(
            src_ref=psi.at[2, :, ba_peer(k)], dst_ref=block_of(a_all, ba, MINE * COMPS),
            send_sem=as_.at[k], recv_sem=ar.at[ba],
            device_id=(ta, ba_peer(k)), device_id_type=MESH,
        )
        for k in range(1, NBA)
    ]
    for copy in applied_sends:
        copy.start()
    pltpu.make_async_copy(psi.at[2, :, ba], block_of(a_all, ba, MINE * COMPS), ar.at[ba]).start()
    cm[...] = jnp.zeros_like(cm)
    for k in range(NBA):
        place = block_of(a_all, ba_peer(k), MINE * COMPS)
        pltpu.make_async_copy(place, place, ar.at[ba_peer(k)]).wait()

    for plane in range(PLANES):
        columns = slice(plane * LANES, (plane + 1) * LANES)
        later = slice(WIDE + plane * LANES, WIDE + (plane + 1) * LANES)
        re = a_all[pl.ds(plane, BLOCK, stride=COMPS), :]
        im = a_all[pl.ds(PLANES + plane, BLOCK, stride=COMPS), :]
        xf[0:BLOCK, columns] = re
        xf[BLOCK : 2 * BLOCK, columns] = im
        (re_hi, re_lo), (im_hi, im_lo) = split(re), split(im)
        x_hi[0:BLOCK, columns] = re_hi
        x_hi[BLOCK : 2 * BLOCK, columns] = im_hi
        x_hi[0:BLOCK, later] = im_hi
        x_hi[BLOCK : 2 * BLOCK, later] = -re_hi
        x_lo[0:BLOCK, columns] = re_lo
        x_lo[BLOCK : 2 * BLOCK, columns] = im_lo
        x_lo[0:BLOCK, later] = im_lo
        x_lo[BLOCK : 2 * BLOCK, later] = -re_lo

    def basis_chunk(k, carry):
        source = lax.rem(ba + k, NBA)
        place = block_of(basis_all, source, GROUP * COMPS)
        pltpu.make_async_copy(place, place, br.at[source]).wait()
        highs, lows = [], []
        for c in range(COMPS):
            part = basis_all[pl.ds(source * (GROUP * COMPS) + c, GROUP, stride=COMPS), :]
            hi, lo = split(part)
            highs.append(hi)
            lows.append(lo)
            rows = pl.ds(pl.multiple_of((c // PLANES) * KEPT + source * GROUP, GROUP), GROUP)
            columns = slice((c % PLANES) * LANES, (c % PLANES + 1) * LANES)
            b_hi[rows, columns] = hi
            b_lo[rows, columns] = lo
        high = jnp.concatenate(highs, axis=1)
        low = jnp.concatenate(lows, axis=1)
        both = matmul(jnp.concatenate([high, low], axis=0), x_hi[...], NT_DIMS)
        total = both[0:GROUP] + both[GROUP : 2 * GROUP] + matmul(high, x_lo[...], NT_DIMS)
        cm[pl.ds(pl.multiple_of(source * GROUP, GROUP), GROUP), 0 : 2 * BLOCK] = total
        return carry

    lax.fori_loop(0, NBA, basis_chunk, 0)

    c_part[...] = cm[...].T[0 : 2 * BLOCK]
    corr_sends = [
        pltpu.make_async_remote_copy(
            src_ref=c_part, dst_ref=c_ba.at[ba], send_sem=cs1.at[k], recv_sem=cr1.at[ba],
            device_id=(ta, ba_peer(k)), device_id_type=MESH,
        )
        for k in range(1, NBA)
    ]
    for copy in corr_sends:
        copy.start()
    c_ba[ba] = c_part[...]
    for k in range(1, NBA):
        pltpu.make_async_copy(c_ba.at[ba_peer(k)], c_ba.at[ba_peer(k)], cr1.at[ba_peer(k)]).wait()
    total = c_ba[0]
    for k in range(1, NBA):
        total = total + c_ba[k]
    c_sum[...] = total
    more_sends = [
        pltpu.make_async_remote_copy(
            src_ref=c_sum, dst_ref=c_ta.at[ta], send_sem=cs2.at[k], recv_sem=cr2.at[ta],
            device_id=(ta_peer(k), ba), device_id_type=MESH,
        )
        for k in range(1, NTA)
    ]
    for copy in more_sends:
        copy.start()
    c_ta[ta] = c_sum[...]
    for k in range(1, NTA):
        pltpu.make_async_copy(c_ta.at[ta_peer(k)], c_ta.at[ta_peer(k)], cr2.at[ta_peer(k)]).wait()
    total = c_ta[0]
    for k in range(1, NTA):
        total = total + c_ta[k]
    norm = 1.0 / (24.0 * 512 * 2 * NTA)
    total = total * norm
    c_full[0 : 2 * BLOCK] = total
    c_re, c_im = split(total[0:BLOCK]), split(total[BLOCK : 2 * BLOCK])
    for level in range(2):
        rows = level * 2 * BLOCK
        wm[rows : rows + BLOCK, 0:KEPT] = c_re[level]
        wm[rows + BLOCK : rows + 2 * BLOCK, 0:KEPT] = c_im[level]
        wm[rows : rows + BLOCK, KEPT : 2 * KEPT] = -c_im[level]
        wm[rows + BLOCK : rows + 2 * BLOCK, KEPT : 2 * KEPT] = c_re[level]

    step = 2 * LANES
    for start in range(0, WIDE, step):
        columns = slice(start, start + step)
        both = matmul(wm[...], b_hi[:, columns], NN_DIMS)
        low = matmul(wm[0 : 2 * BLOCK], b_lo[:, columns], NN_DIMS)
        rest = xf[:, columns] - (both[0 : 2 * BLOCK] + both[2 * BLOCK : 4 * BLOCK] + low)
        hi, lo = split(rest)
        r_hi[:, columns] = hi
        r_lo[:, columns] = lo

    both = matmul(jnp.concatenate([r_hi[...], r_lo[...]], axis=0), r_hi[...], NT_DIMS)
    gram = both[0 : 2 * BLOCK] + both[2 * BLOCK : 4 * BLOCK]
    gram = gram + matmul(r_hi[...], r_lo[...], NT_DIMS)
    vm[...] = jnp.zeros_like(vm)
    vm[:, 0 : 2 * BLOCK] = gram
    lane16 = lax.broadcasted_iota(jnp.int32, (BLOCK, LANES), 1)
    row16 = lax.broadcasted_iota(jnp.int32, (BLOCK, LANES), 0)
    upper, lower = vm[0:BLOCK], vm[BLOCK : 2 * BLOCK]
    turned = jnp.where(lane16 < BLOCK, lroll(lower, LANES - BLOCK), -lroll(lower, BLOCK))
    both = upper + turned
    g_part[...] = jnp.where(lane < 32, both[0:8], lroll(both[8:16], 32))

    gram_sends = [
        pltpu.make_async_remote_copy(
            src_ref=g_part, dst_ref=g_ta.at[ta], send_sem=gs1.at[k], recv_sem=gr1.at[ta],
            device_id=(ta_peer(k), ba), device_id_type=MESH,
        )
        for k in range(1, NTA)
    ]
    for copy in gram_sends:
        copy.start()
    g_ta[ta] = g_part[...]
    c_full[2 * BLOCK : LANES] = jnp.zeros((LANES - 2 * BLOCK, KEPT), F32)
    cm[...] = c_full[...].T
    mine = pl.ds(pl.multiple_of(ba * GROUP, GROUP), GROUP)
    corr[0] = cm[mine, 0:BLOCK]
    corr[1] = cm[mine, BLOCK : 2 * BLOCK]
    for k in range(1, NTA):
        pltpu.make_async_copy(g_ta.at[ta_peer(k)], g_ta.at[ta_peer(k)], gr1.at[ta_peer(k)]).wait()
    total = g_ta[0]
    for k in range(1, NTA):
        total = total + g_ta[k]
    g_sum[...] = total
    gram_more = [
        pltpu.make_async_remote_copy(
            src_ref=g_sum, dst_ref=g_ba.at[ba], send_sem=gs2.at[k], recv_sem=gr2.at[ba],
            device_id=(ta, ba_peer(k)), device_id_type=MESH,
        )
        for k in range(1, NBA)
    ]
    for copy in gram_more:
        copy.start()
    g_ba[ba] = g_sum[...]
    for k in range(1, NBA):
        pltpu.make_async_copy(g_ba.at[ba_peer(k)], g_ba.at[ba_peer(k)], gr2.at[ba_peer(k)]).wait()
    total = g_ba[0]
    for k in range(1, NBA):
        total = total + g_ba[k]
    total = total * norm

    gram = jnp.concatenate([total, lroll(total, LANES - 32)], axis=0)
    m_re = jnp.where(lane16 < BLOCK, gram, jnp.where(lane16 == row16 + BLOCK, 1.0, 0.0))
    m_im = jnp.where(lane16 < BLOCK, lroll(gram, LANES - BLOCK), 0.0)
    for c in range(BLOCK):
        scale = lax.rsqrt(m_re[c : c + 1, c : c + 1])
        row_re = m_re[c : c + 1, :] * scale
        row_im = m_im[c : c + 1, :] * scale
        f_re = m_re[:, c : c + 1] * scale
        f_im = m_im[:, c : c + 1] * scale
        below_row = row16 > c
        at_row = row16 == c
        new_re = m_re - (f_re * row_re - f_im * row_im)
        new_im = m_im - (f_re * row_im + f_im * row_re)
        m_re = jnp.where(below_row, new_re, jnp.where(at_row, row_re, m_re))
        m_im = jnp.where(below_row, new_im, jnp.where(at_row, row_im, m_im))

    vm[0:BLOCK] = jnp.where(lane16 < BLOCK, lroll(m_re, LANES - BLOCK), m_im)
    vm[BLOCK : 2 * BLOCK] = jnp.where(lane16 < BLOCK, -lroll(m_im, LANES - BLOCK), m_re)
    v_hi, v_lo = split(vm[:, 0 : 2 * BLOCK])
    v_both = jnp.concatenate([v_hi, v_lo], axis=0)
    for start in range(0, WIDE, step):
        columns = slice(start, start + step)
        both = matmul(v_both, r_hi[:, columns], NN_DIMS)
        low = matmul(v_hi, r_lo[:, columns], NN_DIMS)
        ortho = both[0 : 2 * BLOCK] + both[2 * BLOCK : 4 * BLOCK] + low
        for offset in range(0, step, LANES):
            plane = (start + offset) // LANES
            for ri in range(2):
                part = ortho[ri * BLOCK : (ri + 1) * BLOCK, offset : offset + LANES]
                osend[pl.ds(ri * PLANES + plane, BLOCK, stride=COMPS), :] = part

    out_sends = [
        pltpu.make_async_remote_copy(
            src_ref=block_of(osend, ba_peer(k), MINE * COMPS), dst_ref=out.at[:, ba],
            send_sem=os_.at[k], recv_sem=or_.at[ba],
            device_id=(ta, ba_peer(k)), device_id_type=MESH,
        )
        for k in range(1, NBA)
    ]
    for copy in out_sends:
        copy.start()
    pltpu.make_async_copy(block_of(osend, ba, MINE * COMPS), out.at[:, ba], or_.at[ba]).start()
    for copy in (*first_halo, *second_halo, *basis_sends, *applied_sends, *corr_sends, *more_sends):
        copy.wait_send()
    for copy in (*gram_sends, *gram_more, *out_sends):
        copy.wait_send()
    for k in range(NBA):
        place = block_of(osend, ba_peer(k), MINE * COMPS)
        pltpu.make_async_copy(place, out.at[:, ba_peer(k)], or_.at[ba_peer(k)]).wait()


def tiles(array):
    times, sites = array.shape[-2:]
    split_up = array.reshape(*array.shape[:-1], sites // LANES, LANES)
    return jnp.swapaxes(split_up, -3, -2).reshape(-1, times * (sites // LANES), LANES)


def untiles(array, shape):
    *lead, times, sites = shape
    split_up = array.reshape(*lead, sites // LANES, times, LANES)
    return jnp.swapaxes(split_up, -3, -2).reshape(shape)


def per_device(search_block, kept_basis, gauge_links, clover_term):
    anywhere = pl.BlockSpec(memory_space=pl.ANY)
    in_vmem = pl.BlockSpec(memory_space=pltpu.VMEM)
    dma = pltpu.SemaphoreType.DMA
    vmem = pltpu.VMEM
    two = 2 * BLOCK
    scratch = [
        vmem((3, MINE * COMPS, 8, LANES), F32),
        vmem((72, 8, LANES), F32),
        vmem((144, 8, LANES), F32),
        vmem((MINE * COMPS, 8, LANES), F32),
        vmem((MINE * 12, 8, LANES), F32),
        vmem((MINE * 12, 8, LANES), F32),
        vmem((2, 12, 8, LANES), F32),
        vmem((2, 12, 8, LANES), F32),
        vmem((2, 12, 8, LANES), F32),
        vmem((2, 12, 8, LANES), F32),
        vmem((KEPT * COMPS, LANES), F32),
        vmem((2 * KEPT, WIDE), BF16),
        vmem((2 * KEPT, WIDE), BF16),
        vmem((BLOCK * COMPS, LANES), F32),
        vmem((two, WIDE), F32),
        vmem((two, 2 * WIDE), BF16),
        vmem((two, 2 * WIDE), BF16),
        vmem((KEPT, LANES), F32),
        vmem((two, KEPT), F32),
        vmem((NBA, two, KEPT), F32),
        vmem((two, KEPT), F32),
        vmem((NTA, two, KEPT), F32),
        vmem((LANES, KEPT), F32),
        vmem((2 * two, 2 * KEPT), BF16),
        vmem((two, WIDE), BF16),
        vmem((two, WIDE), BF16),
        vmem((8, LANES), F32),
        vmem((NTA, 8, LANES), F32),
        vmem((8, LANES), F32),
        vmem((NBA, 8, LANES), F32),
        vmem((two, LANES), F32),
        vmem((BLOCK * COMPS, LANES), F32),
        dma((3,)), dma((2, 2)), dma((2, 2)),
        dma((NBA,)), dma((NBA,)), dma((NBA,)), dma((NBA,)), dma((NBA,)), dma((NBA,)),
        dma((NTA,)), dma((NTA,)), dma((NTA,)), dma((NTA,)),
        dma((NBA,)), dma((NBA,)), dma((NBA,)), dma((NBA,)),
    ]
    ortho, correlations = pl.pallas_call(
        kernel,
        out_shape=(
            jax.ShapeDtypeStruct((MINE * COMPS, 8, LANES), F32),
            jax.ShapeDtypeStruct((2, GROUP, BLOCK), F32),
        ),
        in_specs=[anywhere] * 4,
        out_specs=(in_vmem, in_vmem),
        scratch_shapes=scratch,
        compiler_params=pltpu.CompilerParams(
            collective_id=0, has_side_effects=True, vmem_limit_bytes=56 * 1024 * 1024
        ),
    )(tiles(search_block), tiles(kept_basis), tiles(gauge_links), tiles(clover_term))
    slab = search_block.shape[-2:]
    return untiles(ortho, (MINE, 2, 4, 3, *slab)), correlations


def solution(mesh):
    over_time = P(None, None, None, None, "ta", None)
    grouped = P("ba", None, None, None, "ta", None)
    return jax.shard_map(
        per_device,
        mesh=mesh,
        in_specs=(over_time, grouped, over_time, over_time),
        out_specs=(grouped, P(None, "ba", None)),
        check_vma=False,
    )
```

```python
import jax
import jax.numpy as jnp
from jax import lax
from jax.experimental import pallas as pl
from jax.experimental.pallas import tpu as pltpu
from jax.sharding import PartitionSpec as P

MESH = pl.DeviceIdType.MESH
F32 = jnp.float32
BF16 = jnp.bfloat16

HOPPING = 0.13
NTA, NBA = 16, 8
BLOCK = 16
KEPT = 128
GROUP = KEPT // NBA
MINE = BLOCK // NBA
COMPS = 24
PLANES = 12
LANES = 128
WIDE = PLANES * LANES

PIECES = 2
ORDER = (
    ((1, 0), (0, 1), (3, 0), (1, 1), (2, 0), (3, 1), (2, 1)),
    ((0, 1), (3, 0), (1, 1), (1, 0), (3, 1), (2, 1), (2, 0)),
)
PACE = (3, 0, 4, 0, 7)

ISIGMA = (
    ((1, True, 1), (0, True, 1)),
    ((1, False, 1), (0, False, -1)),
    ((0, True, 1), (1, True, -1)),
)

NT_DIMS = (((1,), (1,)), ((), ()))
NN_DIMS = (((1,), (0,)), ((), ()))


def split(value):
    high = value.astype(BF16)
    return high, (value - high.astype(F32)).astype(BF16)


def matmul(left, right, dims):
    return lax.dot_general(left, right, dims, preferred_element_type=F32)


def comp(ri, spin, colour):
    return ri * 12 + spin * 3 + colour


def half(ri, spin, colour):
    return ri * 6 + spin * 3 + colour


def add_phase(base, other, imag, sign):
    if imag:
        other = (other[1], other[0])
        signs = (-sign, sign)
    else:
        signs = (sign, sign)
    return tuple(b + o if s > 0 else b - o for b, o, s in zip(base, other, signs))


def kernel(
    search, basis, links, clover, out, corr,
    psi, lk, cl, acc, h_t, b_t, dn, up, rdn, rup,
    basis_all, b_hi, b_lo, a_all, xf, x_hi, x_lo, cm, c_part, c_sum, c_ba, c_ta, c_full,
    wm, r_hi, r_lo, g_part, g_ta, g_sum, g_ba, vm, osend,
    in_sem, hs, hr, bs, br, as_, ar, cs, cr, gs1, gr1, gs2, gr2, os_, or_,
):
    ta = lax.axis_index("ta")
    ba = lax.axis_index("ba")
    above = (lax.rem(ta + 1, NTA), ba)
    below = (lax.rem(ta + NTA - 1, NTA), ba)

    def ta_peer(k):
        return lax.rem(ta + k, NTA)

    def ba_peer(k):
        return lax.rem(ba + k, NBA)

    barrier = pltpu.get_barrier_semaphore()
    for k in range(1, NTA):
        pl.semaphore_signal(barrier, inc=1, device_id=(ta_peer(k), ba), device_id_type=MESH)
    for k in range(1, NBA):
        pl.semaphore_signal(barrier, inc=1, device_id=(ta, ba_peer(k)), device_id_type=MESH)

    own = pl.multiple_of(ba * MINE * COMPS, 8)
    load_psi = pltpu.make_async_copy(
        search.at[pl.ds(own, MINE * COMPS)], psi.at[0], in_sem.at[0]
    )
    load_links = pltpu.make_async_copy(links, lk, in_sem.at[1])
    load_clover = pltpu.make_async_copy(clover, cl, in_sem.at[2])
    load_basis = pltpu.make_async_copy(basis.at[:, ba], basis_all.at[pl.ds(pl.multiple_of(ba * GROUP * COMPS, 8), GROUP * COMPS)], br.at[ba])
    load_psi.start()
    load_links.start()
    load_clover.start()
    load_basis.start()

    lane = lax.broadcasted_iota(jnp.int32, (8, LANES), 1)
    sub = lax.broadcasted_iota(jnp.int32, (8, LANES), 0)
    z_lane = lane % 8
    y_lane = (lane // 8) % 8
    z_last, z_first = z_lane == 7, z_lane == 0
    y_last, y_first = y_lane == 7, y_lane == 0
    x_even = lane < 64
    t_odd = sub % 2 == 1
    sign_last = jnp.where(ta == NTA - 1, -1.0, 1.0).astype(F32)
    sign_first = jnp.where(ta == 0, -1.0, 1.0).astype(F32)

    def lroll(value, shift):
        return pltpu.roll(value, shift, 1)

    def sroll(value, shift):
        return pltpu.roll(value, shift, 0)

    def ahead(value, mu):
        if mu == 0:
            turned = lroll(value, 64)
            return jnp.where(x_even, turned, sroll(turned, 6))
        if mu == 1:
            return jnp.where(y_last, lroll(value, 56), lroll(value, 120))
        return jnp.where(z_last, lroll(value, 7), lroll(value, 127))

    def behind(value, mu):
        if mu == 0:
            turned = lroll(value, 64)
            return jnp.where(x_even, sroll(turned, 2), turned)
        if mu == 1:
            return jnp.where(y_first, lroll(value, 72), lroll(value, 8))
        return jnp.where(z_first, lroll(value, 121), lroll(value, 1))

    def link(mu, row, col):
        place = mu * 18 + row * 3 + col
        return lk[place], lk[place + 9]

    def times_link(mu, vec):
        result = []
        for row in range(3):
            re = im = None
            for col in range(3):
                ur, ui = link(mu, row, col)
                vr, vi = vec[col]
                tr, ti = ur * vr - ui * vi, ur * vi + ui * vr
                re, im = (tr, ti) if re is None else (re + tr, im + ti)
            result.append((re, im))
        return result

    def times_dagger(mu, vec):
        result = []
        for row in range(3):
            re = im = None
            for col in range(3):
                ur, ui = link(mu, col, row)
                vr, vi = vec[col]
                tr, ti = ur * vr + ui * vi, ur * vi - ui * vr
                re, im = (tr, ti) if re is None else (re + tr, im + ti)
            result.append((re, im))
        return result

    def time_prepare(a):
        def one(v, carry):
            def field(spin, colour):
                base = v * COMPS
                return psi[a, base + comp(0, spin, colour)], psi[a, base + comp(1, spin, colour)]

            for spin in range(2):
                sums = []
                for colour in range(3):
                    upper, lower = field(spin, colour), field(spin + 2, colour)
                    for ri in range(2):
                        h_t[v * 12 + half(ri, spin, colour)] = upper[ri] - lower[ri]
                    sums.append((upper[0] + lower[0], upper[1] + lower[1]))
                linked = times_dagger(3, sums)
                for colour in range(3):
                    for ri in range(2):
                        b_t[v * 12 + half(ri, spin, colour)] = linked[colour][ri]
            return carry

        lax.fori_loop(0, MINE, one, 0)
        for i in range(12):
            dn[a, i] = jnp.where(t_odd, sroll(h_t[12 + i], 1), h_t[i])
            up[a, i] = jnp.where(t_odd, b_t[12 + i], sroll(b_t[i], 7))

    def halo_copies(a):
        down = pltpu.make_async_remote_copy(
            src_ref=dn.at[a], dst_ref=rdn.at[a], send_sem=hs.at[a, 0], recv_sem=hr.at[a, 0],
            device_id=below, device_id_type=MESH,
        )
        upward = pltpu.make_async_remote_copy(
            src_ref=up.at[a], dst_ref=rup.at[a], send_sem=hs.at[a, 1], recv_sem=hr.at[a, 1],
            device_id=above, device_id_type=MESH,
        )
        return down, upward

    def local_part(a):
        def one(v, carry):
            base = v * COMPS

            def field(spin, colour):
                return psi[a, base + comp(0, spin, colour)], psi[a, base + comp(1, spin, colour)]

            for chiral in range(2):
                vec = [field(2 * chiral + i // 3, i % 3) for i in range(6)]
                for row in range(6):
                    re = im = None
                    for col in range(6):
                        place = chiral * 72 + row * 6 + col
                        cr, ci = cl[place], cl[place + 36]
                        vr, vi = vec[col]
                        tr, ti = cr * vr - ci * vi, cr * vi + ci * vr
                        re, im = (tr, ti) if re is None else (re + tr, im + ti)
                    spin = 2 * chiral + row // 3
                    acc[base + comp(0, spin, row % 3)] = re
                    acc[base + comp(1, spin, row % 3)] = im
            for mu in range(3):
                for spin in range(2):
                    source, imag, sign = ISIGMA[mu][spin]
                    forward, backward = [], []
                    for colour in range(3):
                        upper, lower = field(spin, colour), field(2 + source, colour)
                        minus = add_phase(upper, lower, imag, sign)
                        plus = add_phase(upper, lower, imag, -sign)
                        forward.append(tuple(ahead(value, mu) for value in minus))
                        backward.append(plus)
                    forward = times_link(mu, forward)
                    backward = times_dagger(mu, backward)
                    backward = [tuple(behind(value, mu) for value in pair) for pair in backward]
                    target = [s for s in range(2) if ISIGMA[mu][s][0] == spin][0]
                    _, imag, sign = ISIGMA[mu][target]
                    for colour in range(3):
                        f, b = forward[colour], backward[colour]
                        for ri in range(2):
                            place = base + comp(ri, spin, colour)
                            acc[place] = acc[place] + (f[ri] + b[ri])
                        places = [base + comp(ri, 2 + target, colour) for ri in range(2)]
                        total = add_phase(
                            (acc[places[0]], acc[places[1]]), (b[0] - f[0], b[1] - f[1]), imag, sign
                        )
                        acc[places[0]] = total[0]
                        acc[places[1]] = total[1]
            return carry

        lax.fori_loop(0, MINE, one, 0)

    def time_finish(a):
        for v in range(MINE):
            for spin in range(2):
                front, back = [], []
                for colour in range(3):
                    f, b = [], []
                    for ri in range(2):
                        i = half(ri, spin, colour)
                        got, low = rdn[a, i] * sign_last, rup[a, i] * sign_first
                        got = sroll(got, 1) if v == 0 else got
                        low = low if v == 0 else sroll(low, 7)
                        f.append(jnp.where(t_odd, got, sroll(h_t[v * 12 + i], 7)))
                        b.append(jnp.where(t_odd, sroll(b_t[v * 12 + i], 1), low))
                    front.append(tuple(f))
                    back.append(tuple(b))
                front = times_link(3, front)
                for colour in range(3):
                    for ri in range(2):
                        f, b = front[colour][ri], back[colour][ri]
                        upper = v * COMPS + comp(ri, spin, colour)
                        lower = v * COMPS + comp(ri, spin + 2, colour)
                        psi[a + 1, upper] = acc[upper] + (f + b)
                        psi[a + 1, lower] = (f - b) - acc[lower]

    load_psi.wait()
    load_links.wait()

    def scale_link(i, carry):
        lk[i] = lk[i] * (-HOPPING)
        return carry

    lax.fori_loop(0, 72, scale_link, 0)
    time_prepare(0)
    load_clover.wait()
    local_part(0)

    pl.semaphore_wait(barrier, NTA + NBA - 2)

    first_halo = halo_copies(0)
    for copy in first_halo:
        copy.start()

    def block_of(ref, place, size):
        return ref.at[pl.ds(pl.multiple_of(place * size, 8), size)]

    core = lax.rem(ta, 2)
    z_place, x_place = ba // 2, lax.rem(ba, 2)
    piece_rows = GROUP * COMPS // PIECES
    queue = [(step, piece) for step in range(NBA - 1) for piece in range(PIECES)]

    def send_basis(count):
        for step, piece in queue[:count]:
            (z_even, x_even_core), (z_odd, x_odd_core) = ORDER[0][step], ORDER[1][step]
            dz = jnp.where(core == 0, z_even, z_odd)
            dx = jnp.where(core == 0, x_even_core, x_odd_core)
            to = lax.rem(z_place + dz, NBA // 2) * 2 + lax.rem(x_place + dx, 2)
            start = pl.multiple_of(ba * (GROUP * COMPS) + piece * piece_rows, 8)
            pltpu.make_async_remote_copy(
                src_ref=basis.at[pl.ds(piece * piece_rows, piece_rows), to],
                dst_ref=basis_all.at[pl.ds(start, piece_rows)],
                send_sem=bs, recv_sem=br.at[ba],
                device_id=(ta, to), device_id_type=MESH,
            ).start()
        del queue[:count]

    send_basis(PACE[0])
    for copy in first_halo:
        copy.wait_recv()
    send_basis(PACE[1])
    time_finish(0)
    time_prepare(1)
    second_halo = halo_copies(1)
    for copy in second_halo:
        copy.start()
    send_basis(PACE[2])
    local_part(1)
    send_basis(PACE[3])
    for copy in second_halo:
        copy.wait_recv()
    time_finish(1)

    applied_sends = [
        pltpu.make_async_remote_copy(
            src_ref=psi.at[2, :, ba_peer(k)], dst_ref=block_of(a_all, ba, MINE * COMPS),
            send_sem=as_.at[k], recv_sem=ar.at[ba],
            device_id=(ta, ba_peer(k)), device_id_type=MESH,
        )
        for k in range(1, NBA)
    ]
    for copy in applied_sends:
        copy.start()
    send_basis(PACE[4])
    pltpu.make_async_copy(psi.at[2, :, ba], block_of(a_all, ba, MINE * COMPS), ar.at[ba]).start()
    cm[...] = jnp.zeros_like(cm)
    for k in range(NBA):
        place = block_of(a_all, ba_peer(k), MINE * COMPS)
        pltpu.make_async_copy(place, place, ar.at[ba_peer(k)]).wait()

    for plane in range(PLANES):
        columns = slice(plane * LANES, (plane + 1) * LANES)
        later = slice(WIDE + plane * LANES, WIDE + (plane + 1) * LANES)
        re = a_all[pl.ds(plane, BLOCK, stride=COMPS), :]
        im = a_all[pl.ds(PLANES + plane, BLOCK, stride=COMPS), :]
        xf[0:BLOCK, columns] = re
        xf[BLOCK : 2 * BLOCK, columns] = im
        (re_hi, re_lo), (im_hi, im_lo) = split(re), split(im)
        x_hi[0:BLOCK, columns] = re_hi
        x_hi[BLOCK : 2 * BLOCK, columns] = im_hi
        x_hi[0:BLOCK, later] = im_hi
        x_hi[BLOCK : 2 * BLOCK, later] = -re_hi
        x_lo[0:BLOCK, columns] = re_lo
        x_lo[BLOCK : 2 * BLOCK, columns] = im_lo
        x_lo[0:BLOCK, later] = im_lo
        x_lo[BLOCK : 2 * BLOCK, later] = -re_lo

    def basis_chunk(k, carry):
        source = lax.rem(ba + k, NBA)
        place = block_of(basis_all, source, GROUP * COMPS)
        pltpu.make_async_copy(place, place, br.at[source]).wait()
        highs, lows = [], []
        for c in range(COMPS):
            part = basis_all[pl.ds(source * (GROUP * COMPS) + c, GROUP, stride=COMPS), :]
            hi, lo = split(part)
            highs.append(hi)
            lows.append(lo)
            rows = pl.ds(pl.multiple_of((c // PLANES) * KEPT + source * GROUP, GROUP), GROUP)
            columns = slice((c % PLANES) * LANES, (c % PLANES + 1) * LANES)
            b_hi[rows, columns] = hi
            b_lo[rows, columns] = lo
        high = jnp.concatenate(highs, axis=1)
        low = jnp.concatenate(lows, axis=1)
        both = matmul(jnp.concatenate([high, low], axis=0), x_hi[...], NT_DIMS)
        total = both[0:GROUP] + both[GROUP : 2 * GROUP] + matmul(high, x_lo[...], NT_DIMS)
        cm[pl.ds(pl.multiple_of(source * GROUP, GROUP), GROUP), 0 : 2 * BLOCK] = total
        return carry

    lax.fori_loop(0, NBA, basis_chunk, 0)

    def all_of(ref, sem):
        pltpu.make_async_copy(ref, ref, sem).wait()

    c_part[...] = cm[...].T[0 : 2 * BLOCK]
    for k in range(1, NBA):
        pltpu.make_async_remote_copy(
            src_ref=c_part, dst_ref=c_ba.at[ba], send_sem=cs.at[0], recv_sem=cr.at[0],
            device_id=(ta, ba_peer(k)), device_id_type=MESH,
        ).start()
    c_ba[ba] = c_part[...]
    all_of(c_ba.at[pl.ds(0, NBA - 1)], cr.at[0])
    total = c_ba[0]
    for k in range(1, NBA):
        total = total + c_ba[k]
    c_sum[...] = total
    for k in range(1, NTA):
        pltpu.make_async_remote_copy(
            src_ref=c_sum, dst_ref=c_ta.at[ta], send_sem=cs.at[1], recv_sem=cr.at[1],
            device_id=(ta_peer(k), ba), device_id_type=MESH,
        ).start()
    c_ta[ta] = c_sum[...]
    all_of(c_ta.at[pl.ds(0, NTA - 1)], cr.at[1])
    total = c_ta[0]
    for k in range(1, NTA):
        total = total + c_ta[k]
    norm = 1.0 / (24.0 * 512 * 2 * NTA)
    total = total * norm
    c_full[0 : 2 * BLOCK] = total
    c_re, c_im = split(total[0:BLOCK]), split(total[BLOCK : 2 * BLOCK])
    for level in range(2):
        rows = level * 2 * BLOCK
        wm[rows : rows + BLOCK, 0:KEPT] = c_re[level]
        wm[rows + BLOCK : rows + 2 * BLOCK, 0:KEPT] = c_im[level]
        wm[rows : rows + BLOCK, KEPT : 2 * KEPT] = -c_im[level]
        wm[rows + BLOCK : rows + 2 * BLOCK, KEPT : 2 * KEPT] = c_re[level]

    step = 2 * LANES
    for start in range(0, WIDE, step):
        columns = slice(start, start + step)
        both = matmul(wm[...], b_hi[:, columns], NN_DIMS)
        low = matmul(wm[0 : 2 * BLOCK], b_lo[:, columns], NN_DIMS)
        rest = xf[:, columns] - (both[0 : 2 * BLOCK] + both[2 * BLOCK : 4 * BLOCK] + low)
        hi, lo = split(rest)
        r_hi[:, columns] = hi
        r_lo[:, columns] = lo

    both = matmul(jnp.concatenate([r_hi[...], r_lo[...]], axis=0), r_hi[...], NT_DIMS)
    gram = both[0 : 2 * BLOCK] + both[2 * BLOCK : 4 * BLOCK]
    gram = gram + matmul(r_hi[...], r_lo[...], NT_DIMS)
    vm[...] = jnp.zeros_like(vm)
    vm[:, 0 : 2 * BLOCK] = gram
    lane16 = lax.broadcasted_iota(jnp.int32, (BLOCK, LANES), 1)
    row16 = lax.broadcasted_iota(jnp.int32, (BLOCK, LANES), 0)
    upper, lower = vm[0:BLOCK], vm[BLOCK : 2 * BLOCK]
    turned = jnp.where(lane16 < BLOCK, lroll(lower, LANES - BLOCK), -lroll(lower, BLOCK))
    both = upper + turned
    g_part[...] = jnp.where(lane < 32, both[0:8], lroll(both[8:16], 32))

    for k in range(1, NTA):
        pltpu.make_async_remote_copy(
            src_ref=g_part, dst_ref=g_ta.at[ta], send_sem=gs1, recv_sem=gr1,
            device_id=(ta_peer(k), ba), device_id_type=MESH,
        ).start()
    g_ta[ta] = g_part[...]
    mine = pl.ds(pl.multiple_of(ba * GROUP, GROUP), GROUP)
    c_full[2 * BLOCK : LANES] = jnp.zeros((LANES - 2 * BLOCK, KEPT), F32)
    cm[...] = c_full[...].T
    corr[0] = cm[mine, 0:BLOCK]
    corr[1] = cm[mine, BLOCK : 2 * BLOCK]
    all_of(g_ta.at[pl.ds(0, NTA - 1)], gr1)
    total = g_ta[0]
    for k in range(1, NTA):
        total = total + g_ta[k]
    g_sum[...] = total
    for k in range(1, NBA):
        pltpu.make_async_remote_copy(
            src_ref=g_sum, dst_ref=g_ba.at[ba], send_sem=gs2, recv_sem=gr2,
            device_id=(ta, ba_peer(k)), device_id_type=MESH,
        ).start()
    g_ba[ba] = g_sum[...]
    all_of(g_ba.at[pl.ds(0, NBA - 1)], gr2)
    total = g_ba[0]
    for k in range(1, NBA):
        total = total + g_ba[k]
    total = total * norm

    gram = jnp.concatenate([total, lroll(total, LANES - 32)], axis=0)
    m_re = jnp.where(lane16 < BLOCK, gram, jnp.where(lane16 == row16 + BLOCK, 1.0, 0.0))
    m_im = jnp.where(lane16 < BLOCK, lroll(gram, LANES - BLOCK), 0.0)
    for c in range(BLOCK):
        scale = lax.rsqrt(m_re[c : c + 1, c : c + 1])
        row_re = m_re[c : c + 1, :] * scale
        row_im = m_im[c : c + 1, :] * scale
        f_re = m_re[:, c : c + 1] * scale
        f_im = m_im[:, c : c + 1] * scale
        below_row = row16 > c
        at_row = row16 == c
        new_re = m_re - (f_re * row_re - f_im * row_im)
        new_im = m_im - (f_re * row_im + f_im * row_re)
        m_re = jnp.where(below_row, new_re, jnp.where(at_row, row_re, m_re))
        m_im = jnp.where(below_row, new_im, jnp.where(at_row, row_im, m_im))

    vm[0:BLOCK] = jnp.where(lane16 < BLOCK, lroll(m_re, LANES - BLOCK), m_im)
    vm[BLOCK : 2 * BLOCK] = jnp.where(lane16 < BLOCK, -lroll(m_im, LANES - BLOCK), m_re)
    v_hi, v_lo = split(vm[:, 0 : 2 * BLOCK])
    v_both = jnp.concatenate([v_hi, v_lo], axis=0)
    for start in range(0, WIDE, step):
        columns = slice(start, start + step)
        both = matmul(v_both, r_hi[:, columns], NN_DIMS)
        low = matmul(v_hi, r_lo[:, columns], NN_DIMS)
        ortho = both[0 : 2 * BLOCK] + both[2 * BLOCK : 4 * BLOCK] + low
        for offset in range(0, step, LANES):
            plane = (start + offset) // LANES
            for ri in range(2):
                part = ortho[ri * BLOCK : (ri + 1) * BLOCK, offset : offset + LANES]
                osend[pl.ds(ri * PLANES + plane, BLOCK, stride=COMPS), :] = part

    for k in range(1, NBA):
        pltpu.make_async_remote_copy(
            src_ref=block_of(osend, ba_peer(k), MINE * COMPS), dst_ref=out.at[:, ba],
            send_sem=os_, recv_sem=or_.at[ba],
            device_id=(ta, ba_peer(k)), device_id_type=MESH,
        ).start()
    pltpu.make_async_copy(block_of(osend, ba, MINE * COMPS), out.at[:, ba], or_.at[ba]).start()
    for copy in (*first_halo, *second_halo, *applied_sends):
        copy.wait_send()
    all_of(basis_all.at[pl.ds(0, (NBA - 1) * GROUP * COMPS)], bs)
    all_of(c_ba.at[pl.ds(0, NBA - 1)], cs.at[0])
    all_of(c_ta.at[pl.ds(0, NTA - 1)], cs.at[1])
    all_of(g_ta.at[pl.ds(0, NTA - 1)], gs1)
    all_of(g_ba.at[pl.ds(0, NBA - 1)], gs2)
    all_of(osend.at[pl.ds(0, (NBA - 1) * MINE * COMPS)], os_)
    for k in range(NBA):
        place = block_of(osend, ba_peer(k), MINE * COMPS)
        pltpu.make_async_copy(place, out.at[:, ba_peer(k)], or_.at[ba_peer(k)]).wait()


def tiles(array):
    times, sites = array.shape[-2:]
    split_up = array.reshape(*array.shape[:-1], sites // LANES, LANES)
    return jnp.swapaxes(split_up, -3, -2).reshape(-1, times * (sites // LANES), LANES)


def untiles(array, shape):
    *lead, times, sites = shape
    split_up = array.reshape(*lead, sites // LANES, times, LANES)
    return jnp.swapaxes(split_up, -3, -2).reshape(shape)


def per_device(search_block, kept_basis, gauge_links, clover_term):
    anywhere = pl.BlockSpec(memory_space=pl.ANY)
    in_vmem = pl.BlockSpec(memory_space=pltpu.VMEM)
    dma = pltpu.SemaphoreType.DMA
    vmem = pltpu.VMEM
    two = 2 * BLOCK
    scratch = [
        vmem((3, MINE * COMPS, 8, LANES), F32),
        vmem((72, 8, LANES), F32),
        vmem((144, 8, LANES), F32),
        vmem((MINE * COMPS, 8, LANES), F32),
        vmem((MINE * 12, 8, LANES), F32),
        vmem((MINE * 12, 8, LANES), F32),
        vmem((2, 12, 8, LANES), F32),
        vmem((2, 12, 8, LANES), F32),
        vmem((2, 12, 8, LANES), F32),
        vmem((2, 12, 8, LANES), F32),
        vmem((KEPT * COMPS, LANES), F32),
        vmem((2 * KEPT, WIDE), BF16),
        vmem((2 * KEPT, WIDE), BF16),
        vmem((BLOCK * COMPS, LANES), F32),
        vmem((two, WIDE), F32),
        vmem((two, 2 * WIDE), BF16),
        vmem((two, 2 * WIDE), BF16),
        vmem((KEPT, LANES), F32),
        vmem((two, KEPT), F32),
        vmem((two, KEPT), F32),
        vmem((NBA, two, KEPT), F32),
        vmem((NTA, two, KEPT), F32),
        vmem((LANES, KEPT), F32),
        vmem((2 * two, 2 * KEPT), BF16),
        vmem((two, WIDE), BF16),
        vmem((two, WIDE), BF16),
        vmem((8, LANES), F32),
        vmem((NTA, 8, LANES), F32),
        vmem((8, LANES), F32),
        vmem((NBA, 8, LANES), F32),
        vmem((two, LANES), F32),
        vmem((BLOCK * COMPS, LANES), F32),
        dma((3,)), dma((2, 2)), dma((2, 2)),
        dma, dma((NBA,)), dma((NBA,)), dma((NBA,)), dma((2,)), dma((2,)),
        dma, dma, dma, dma, dma, dma((NBA,)),
    ]
    ortho, correlations = pl.pallas_call(
        kernel,
        out_shape=(
            jax.ShapeDtypeStruct((MINE * COMPS, 8, LANES), F32),
            jax.ShapeDtypeStruct((2, GROUP, BLOCK), F32),
        ),
        in_specs=[anywhere] * 4,
        out_specs=(in_vmem, in_vmem),
        scratch_shapes=scratch,
        compiler_params=pltpu.CompilerParams(
            collective_id=0, has_side_effects=True, vmem_limit_bytes=56 * 1024 * 1024
        ),
    )(tiles(search_block), tiles(kept_basis), tiles(gauge_links), tiles(clover_term))
    slab = search_block.shape[-2:]
    return untiles(ortho, (MINE, 2, 4, 3, *slab)), correlations


def solution(mesh):
    over_time = P(None, None, None, None, "ta", None)
    grouped = P("ba", None, None, None, "ta", None)
    return jax.shard_map(
        per_device,
        mesh=mesh,
        in_specs=(over_time, grouped, over_time, over_time),
        out_specs=(grouped, P(None, "ba", None)),
        check_vma=False,
    )
```

```python
import jax
import jax.numpy as jnp
from jax import lax
from jax.experimental import pallas as pl
from jax.experimental.pallas import tpu as pltpu
from jax.sharding import PartitionSpec as P

MESH = pl.DeviceIdType.MESH
F32 = jnp.float32
BF16 = jnp.bfloat16

HOPPING = 0.13
NTA, NBA = 16, 8
BLOCK = 16
KEPT = 128
GROUP = KEPT // NBA
MINE = BLOCK // NBA
COMPS = 24
PLANES = 12
LANES = 128
WIDE = PLANES * LANES

PIECES = 2
ORDER = (
    ((2, 1), (2, 0), (1, 1), (3, 1), (1, 0), (3, 0), (0, 1)),
    ((2, 0), (2, 1), (3, 1), (1, 1), (1, 0), (0, 1), (3, 0)),
)
PACE = (3, 0, 4, 0, 7)
EARLY = 3

ISIGMA = (
    ((1, True, 1), (0, True, 1)),
    ((1, False, 1), (0, False, -1)),
    ((0, True, 1), (1, True, -1)),
)

NT_DIMS = (((1,), (1,)), ((), ()))
NN_DIMS = (((1,), (0,)), ((), ()))


def split(value):
    high = value.astype(BF16)
    return high, (value - high.astype(F32)).astype(BF16)


def matmul(left, right, dims):
    return lax.dot_general(left, right, dims, preferred_element_type=F32)


def comp(ri, spin, colour):
    return ri * 12 + spin * 3 + colour


def half(ri, spin, colour):
    return ri * 6 + spin * 3 + colour


def add_phase(base, other, imag, sign):
    if imag:
        other = (other[1], other[0])
        signs = (-sign, sign)
    else:
        signs = (sign, sign)
    return tuple(b + o if s > 0 else b - o for b, o, s in zip(base, other, signs))


def kernel(
    search, basis, links, clover, out, corr,
    psi, lk, cl, acc, h_t, b_t, dn, up, rdn, rup,
    basis_all, b_hi, b_lo, a_all, xf, x_hi, x_lo, cm, c_part, c_sum, c_ba, c_ta, c_full,
    wm, r_hi, r_lo, g_part, g_ta, g_sum, g_ba, vm, osend,
    in_sem, hs, hr, bs, br, as_, ar, cs, cr, gs1, gr1, gs2, gr2, os_, or_,
):
    ta = lax.axis_index("ta")
    ba = lax.axis_index("ba")
    above = (lax.rem(ta + 1, NTA), ba)
    below = (lax.rem(ta + NTA - 1, NTA), ba)

    def ta_peer(k):
        return lax.rem(ta + k, NTA)

    def ba_peer(k):
        return lax.rem(ba + k, NBA)

    barrier = pltpu.get_barrier_semaphore()
    for k in range(1, NTA):
        pl.semaphore_signal(barrier, inc=1, device_id=(ta_peer(k), ba), device_id_type=MESH)
    for k in range(1, NBA):
        pl.semaphore_signal(barrier, inc=1, device_id=(ta, ba_peer(k)), device_id_type=MESH)

    own = pl.multiple_of(ba * MINE * COMPS, 8)
    load_psi = pltpu.make_async_copy(
        search.at[pl.ds(own, MINE * COMPS)], psi.at[0], in_sem.at[0]
    )
    load_links = pltpu.make_async_copy(links, lk, in_sem.at[1])
    load_clover = pltpu.make_async_copy(clover, cl, in_sem.at[2])
    load_basis = pltpu.make_async_copy(basis.at[:, ba], basis_all.at[pl.ds(pl.multiple_of(ba * GROUP * COMPS, 8), GROUP * COMPS)], br.at[ba])
    load_psi.start()
    load_links.start()
    load_clover.start()
    load_basis.start()

    lane = lax.broadcasted_iota(jnp.int32, (8, LANES), 1)
    sub = lax.broadcasted_iota(jnp.int32, (8, LANES), 0)
    z_lane = lane % 8
    y_lane = (lane // 8) % 8
    z_last, z_first = z_lane == 7, z_lane == 0
    y_last, y_first = y_lane == 7, y_lane == 0
    x_even = lane < 64
    t_odd = sub % 2 == 1
    sign_last = jnp.where(ta == NTA - 1, -1.0, 1.0).astype(F32)
    sign_first = jnp.where(ta == 0, -1.0, 1.0).astype(F32)

    def lroll(value, shift):
        return pltpu.roll(value, shift, 1)

    def sroll(value, shift):
        return pltpu.roll(value, shift, 0)

    def ahead(value, mu):
        if mu == 0:
            turned = lroll(value, 64)
            return jnp.where(x_even, turned, sroll(turned, 6))
        if mu == 1:
            return jnp.where(y_last, lroll(value, 56), lroll(value, 120))
        return jnp.where(z_last, lroll(value, 7), lroll(value, 127))

    def behind(value, mu):
        if mu == 0:
            turned = lroll(value, 64)
            return jnp.where(x_even, sroll(turned, 2), turned)
        if mu == 1:
            return jnp.where(y_first, lroll(value, 72), lroll(value, 8))
        return jnp.where(z_first, lroll(value, 121), lroll(value, 1))

    def link(mu, row, col):
        place = mu * 18 + row * 3 + col
        return lk[place], lk[place + 9]

    def times_link(mu, vec):
        result = []
        for row in range(3):
            re = im = None
            for col in range(3):
                ur, ui = link(mu, row, col)
                vr, vi = vec[col]
                tr, ti = ur * vr - ui * vi, ur * vi + ui * vr
                re, im = (tr, ti) if re is None else (re + tr, im + ti)
            result.append((re, im))
        return result

    def times_dagger(mu, vec):
        result = []
        for row in range(3):
            re = im = None
            for col in range(3):
                ur, ui = link(mu, col, row)
                vr, vi = vec[col]
                tr, ti = ur * vr + ui * vi, ur * vi - ui * vr
                re, im = (tr, ti) if re is None else (re + tr, im + ti)
            result.append((re, im))
        return result

    def time_prepare(a):
        def one(v, carry):
            def field(spin, colour):
                base = v * COMPS
                return psi[a, base + comp(0, spin, colour)], psi[a, base + comp(1, spin, colour)]

            for spin in range(2):
                sums = []
                for colour in range(3):
                    upper, lower = field(spin, colour), field(spin + 2, colour)
                    for ri in range(2):
                        h_t[v * 12 + half(ri, spin, colour)] = upper[ri] - lower[ri]
                    sums.append((upper[0] + lower[0], upper[1] + lower[1]))
                linked = times_dagger(3, sums)
                for colour in range(3):
                    for ri in range(2):
                        b_t[v * 12 + half(ri, spin, colour)] = linked[colour][ri]
            return carry

        lax.fori_loop(0, MINE, one, 0)
        for i in range(12):
            dn[a, i] = jnp.where(t_odd, sroll(h_t[12 + i], 1), h_t[i])
            up[a, i] = jnp.where(t_odd, b_t[12 + i], sroll(b_t[i], 7))

    def halo_copies(a):
        down = pltpu.make_async_remote_copy(
            src_ref=dn.at[a], dst_ref=rdn.at[a], send_sem=hs.at[a, 0], recv_sem=hr.at[a, 0],
            device_id=below, device_id_type=MESH,
        )
        upward = pltpu.make_async_remote_copy(
            src_ref=up.at[a], dst_ref=rup.at[a], send_sem=hs.at[a, 1], recv_sem=hr.at[a, 1],
            device_id=above, device_id_type=MESH,
        )
        return down, upward

    def local_part(a):
        def one(v, carry):
            base = v * COMPS

            def field(spin, colour):
                return psi[a, base + comp(0, spin, colour)], psi[a, base + comp(1, spin, colour)]

            for chiral in range(2):
                vec = [field(2 * chiral + i // 3, i % 3) for i in range(6)]
                for row in range(6):
                    re = im = None
                    for col in range(6):
                        place = chiral * 72 + row * 6 + col
                        cr, ci = cl[place], cl[place + 36]
                        vr, vi = vec[col]
                        tr, ti = cr * vr - ci * vi, cr * vi + ci * vr
                        re, im = (tr, ti) if re is None else (re + tr, im + ti)
                    spin = 2 * chiral + row // 3
                    acc[base + comp(0, spin, row % 3)] = re
                    acc[base + comp(1, spin, row % 3)] = im
            for mu in range(3):
                for spin in range(2):
                    source, imag, sign = ISIGMA[mu][spin]
                    forward, backward = [], []
                    for colour in range(3):
                        upper, lower = field(spin, colour), field(2 + source, colour)
                        minus = add_phase(upper, lower, imag, sign)
                        plus = add_phase(upper, lower, imag, -sign)
                        forward.append(tuple(ahead(value, mu) for value in minus))
                        backward.append(plus)
                    forward = times_link(mu, forward)
                    backward = times_dagger(mu, backward)
                    backward = [tuple(behind(value, mu) for value in pair) for pair in backward]
                    target = [s for s in range(2) if ISIGMA[mu][s][0] == spin][0]
                    _, imag, sign = ISIGMA[mu][target]
                    for colour in range(3):
                        f, b = forward[colour], backward[colour]
                        for ri in range(2):
                            place = base + comp(ri, spin, colour)
                            acc[place] = acc[place] + (f[ri] + b[ri])
                        places = [base + comp(ri, 2 + target, colour) for ri in range(2)]
                        total = add_phase(
                            (acc[places[0]], acc[places[1]]), (b[0] - f[0], b[1] - f[1]), imag, sign
                        )
                        acc[places[0]] = total[0]
                        acc[places[1]] = total[1]
            return carry

        lax.fori_loop(0, MINE, one, 0)

    def time_finish(a):
        for v in range(MINE):
            for spin in range(2):
                front, back = [], []
                for colour in range(3):
                    f, b = [], []
                    for ri in range(2):
                        i = half(ri, spin, colour)
                        got, low = rdn[a, i] * sign_last, rup[a, i] * sign_first
                        got = sroll(got, 1) if v == 0 else got
                        low = low if v == 0 else sroll(low, 7)
                        f.append(jnp.where(t_odd, got, sroll(h_t[v * 12 + i], 7)))
                        b.append(jnp.where(t_odd, sroll(b_t[v * 12 + i], 1), low))
                    front.append(tuple(f))
                    back.append(tuple(b))
                front = times_link(3, front)
                for colour in range(3):
                    for ri in range(2):
                        f, b = front[colour][ri], back[colour][ri]
                        upper = v * COMPS + comp(ri, spin, colour)
                        lower = v * COMPS + comp(ri, spin + 2, colour)
                        psi[a + 1, upper] = acc[upper] + (f + b)
                        psi[a + 1, lower] = (f - b) - acc[lower]

    load_psi.wait()
    load_links.wait()

    def scale_link(i, carry):
        lk[i] = lk[i] * (-HOPPING)
        return carry

    lax.fori_loop(0, 72, scale_link, 0)
    time_prepare(0)
    load_clover.wait()
    local_part(0)

    pl.semaphore_wait(barrier, NTA + NBA - 2)

    first_halo = halo_copies(0)
    for copy in first_halo:
        copy.start()

    def block_of(ref, place, size):
        return ref.at[pl.ds(pl.multiple_of(place * size, 8), size)]

    core = lax.rem(ta, 2)
    z_place, x_place = ba // 2, lax.rem(ba, 2)
    piece_rows = GROUP * COMPS // PIECES
    queue = [(step, piece) for step in range(NBA - 1) for piece in range(PIECES)]

    def send_basis(count):
        for step, piece in queue[:count]:
            (z_even, x_even_core), (z_odd, x_odd_core) = ORDER[0][step], ORDER[1][step]
            dz = jnp.where(core == 0, z_even, z_odd)
            dx = jnp.where(core == 0, x_even_core, x_odd_core)
            to = lax.rem(z_place + dz, NBA // 2) * 2 + lax.rem(x_place + dx, 2)
            start = pl.multiple_of(ba * (GROUP * COMPS) + piece * piece_rows, 8)
            pltpu.make_async_remote_copy(
                src_ref=basis.at[pl.ds(piece * piece_rows, piece_rows), to],
                dst_ref=basis_all.at[pl.ds(start, piece_rows)],
                send_sem=bs, recv_sem=br.at[ba],
                device_id=(ta, to), device_id_type=MESH,
            ).start()
        del queue[:count]

    send_basis(PACE[0])
    for copy in first_halo:
        copy.wait_recv()
    send_basis(PACE[1])
    time_finish(0)
    time_prepare(1)
    second_halo = halo_copies(1)
    for copy in second_halo:
        copy.start()
    send_basis(PACE[2])
    local_part(1)
    send_basis(PACE[3])
    for copy in second_halo:
        copy.wait_recv()
    time_finish(1)

    applied_sends = [
        pltpu.make_async_remote_copy(
            src_ref=psi.at[2, :, ba_peer(k)], dst_ref=block_of(a_all, ba, MINE * COMPS),
            send_sem=as_.at[k], recv_sem=ar.at[ba],
            device_id=(ta, ba_peer(k)), device_id_type=MESH,
        )
        for k in range(1, NBA)
    ]
    for copy in applied_sends:
        copy.start()
    send_basis(PACE[4])
    pltpu.make_async_copy(psi.at[2, :, ba], block_of(a_all, ba, MINE * COMPS), ar.at[ba]).start()
    cm[...] = jnp.zeros_like(cm)
    for k in range(NBA):
        place = block_of(a_all, ba_peer(k), MINE * COMPS)
        pltpu.make_async_copy(place, place, ar.at[ba_peer(k)]).wait()

    for plane in range(PLANES):
        columns = slice(plane * LANES, (plane + 1) * LANES)
        later = slice(WIDE + plane * LANES, WIDE + (plane + 1) * LANES)
        re = a_all[pl.ds(plane, BLOCK, stride=COMPS), :]
        im = a_all[pl.ds(PLANES + plane, BLOCK, stride=COMPS), :]
        xf[0:BLOCK, columns] = re
        xf[BLOCK : 2 * BLOCK, columns] = im
        (re_hi, re_lo), (im_hi, im_lo) = split(re), split(im)
        x_hi[0:BLOCK, columns] = re_hi
        x_hi[BLOCK : 2 * BLOCK, columns] = im_hi
        x_hi[0:BLOCK, later] = im_hi
        x_hi[BLOCK : 2 * BLOCK, later] = -re_hi
        x_lo[0:BLOCK, columns] = re_lo
        x_lo[BLOCK : 2 * BLOCK, columns] = im_lo
        x_lo[0:BLOCK, later] = im_lo
        x_lo[BLOCK : 2 * BLOCK, later] = -re_lo

    def source_of(dz, dx):
        return lax.rem(z_place + NBA // 2 - dz, NBA // 2) * 2 + lax.rem(x_place + dx, 2)

    def packed(values, base):
        codes = [sum(value * base**i for i, value in enumerate(row)) for row in values]
        return jnp.where(core == 0, codes[0], codes[1])

    steps = [((0, 0), *order) for order in ORDER]
    z_codes = packed([[step[0] for step in order] for order in steps], 4)
    x_codes = packed([[step[1] for step in order] for order in steps], 2)
    places = packed([[steps[0].index(step) for step in order] for order in steps], 8)

    def basis_chunk(k, carry):
        two_to = sum(jnp.where(k == i, 2**i, 0) for i in range(NBA))
        dz = lax.rem(z_codes // (two_to * two_to), 4)
        spot = lax.rem(places // (two_to * two_to * two_to), 8)
        source = source_of(dz, lax.rem(x_codes // two_to, 2))
        place = block_of(basis_all, source, GROUP * COMPS)
        pltpu.make_async_copy(place, place, br.at[source]).wait()
        highs, lows = [], []
        for c in range(COMPS):
            part = basis_all[pl.ds(source * (GROUP * COMPS) + c, GROUP, stride=COMPS), :]
            hi, lo = split(part)
            highs.append(hi)
            lows.append(lo)
            rows = pl.ds(pl.multiple_of((c // PLANES) * KEPT + source * GROUP, GROUP), GROUP)
            columns = slice((c % PLANES) * LANES, (c % PLANES + 1) * LANES)
            b_hi[rows, columns] = hi
            b_lo[rows, columns] = lo
        high = jnp.concatenate(highs, axis=1)
        low = jnp.concatenate(lows, axis=1)
        both = matmul(jnp.concatenate([high, low], axis=0), x_hi[...], NT_DIMS)
        total = both[0:GROUP] + both[GROUP : 2 * GROUP] + matmul(high, x_lo[...], NT_DIMS)
        cm[0:GROUP, 0 : 2 * BLOCK] = total
        shift = 64 * lax.rem(spot, 2)
        upper, lower = cm[0:8], cm[8:16]
        c_part[spot // 2] = c_part[spot // 2] + (pltpu.roll(upper, shift, 1) + pltpu.roll(lower, shift + 32, 1))
        return carry

    def all_of(ref, sem):
        pltpu.make_async_copy(ref, ref, sem).wait()

    def send_tiles(first, count, sem):
        tiles_of = pl.ds(first, count)
        for k in range(1, NTA):
            pltpu.make_async_remote_copy(
                src_ref=c_part.at[tiles_of], dst_ref=c_ta.at[ta, tiles_of], send_sem=cs.at[sem], recv_sem=cr.at[sem],
                device_id=(ta_peer(k), ba), device_id_type=MESH,
            ).start()
        c_ta[ta, tiles_of] = c_part[tiles_of]

    c_part[...] = jnp.zeros_like(c_part)
    lax.fori_loop(0, 2 * EARLY, basis_chunk, 0)
    send_tiles(0, EARLY, 0)
    lax.fori_loop(2 * EARLY, NBA, basis_chunk, 0)
    send_tiles(EARLY, NBA // 2 - EARLY, 1)

    for first, count, sem in ((0, EARLY, 0), (EARLY, NBA // 2 - EARLY, 1)):
        all_of(c_ta.at[pl.ds(0, NTA - 1), pl.ds(first, count)], cr.at[sem])
        for i in range(first, first + count):
            total = c_ta[0, i]
            for k in range(1, NTA):
                total = total + c_ta[k, i]
            for part in range(4):
                source = source_of(*steps[0][2 * i + part // 2])
                row = pl.multiple_of(source * GROUP + 8 * (part % 2), 8)
                cm[pl.ds(row, 8)] = lroll(total, LANES - 32 * part) if part else total

    c_sum[...] = cm[...].T[0 : 2 * BLOCK]
    for k in range(1, NBA):
        pltpu.make_async_remote_copy(
            src_ref=c_sum, dst_ref=c_ba.at[ba], send_sem=cs.at[2], recv_sem=cr.at[2],
            device_id=(ta, ba_peer(k)), device_id_type=MESH,
        ).start()
    c_ba[ba] = c_sum[...]
    all_of(c_ba.at[pl.ds(0, NBA - 1)], cr.at[2])
    total = c_ba[0]
    for k in range(1, NBA):
        total = total + c_ba[k]
    norm = 1.0 / (24.0 * 512 * 2 * NTA)
    total = total * norm
    c_full[0 : 2 * BLOCK] = total
    c_re, c_im = split(total[0:BLOCK]), split(total[BLOCK : 2 * BLOCK])
    for level in range(2):
        rows = level * 2 * BLOCK
        wm[rows : rows + BLOCK, 0:KEPT] = c_re[level]
        wm[rows + BLOCK : rows + 2 * BLOCK, 0:KEPT] = c_im[level]
        wm[rows : rows + BLOCK, KEPT : 2 * KEPT] = -c_im[level]
        wm[rows + BLOCK : rows + 2 * BLOCK, KEPT : 2 * KEPT] = c_re[level]

    step = 2 * LANES
    for start in range(0, WIDE, step):
        columns = slice(start, start + step)
        both = matmul(wm[...], b_hi[:, columns], NN_DIMS)
        low = matmul(wm[0 : 2 * BLOCK], b_lo[:, columns], NN_DIMS)
        rest = xf[:, columns] - (both[0 : 2 * BLOCK] + both[2 * BLOCK : 4 * BLOCK] + low)
        hi, lo = split(rest)
        r_hi[:, columns] = hi
        r_lo[:, columns] = lo

    both = matmul(jnp.concatenate([r_hi[...], r_lo[...]], axis=0), r_hi[...], NT_DIMS)
    gram = both[0 : 2 * BLOCK] + both[2 * BLOCK : 4 * BLOCK]
    gram = gram + matmul(r_hi[...], r_lo[...], NT_DIMS)
    vm[...] = jnp.zeros_like(vm)
    vm[:, 0 : 2 * BLOCK] = gram
    lane16 = lax.broadcasted_iota(jnp.int32, (BLOCK, LANES), 1)
    row16 = lax.broadcasted_iota(jnp.int32, (BLOCK, LANES), 0)
    upper, lower = vm[0:BLOCK], vm[BLOCK : 2 * BLOCK]
    turned = jnp.where(lane16 < BLOCK, lroll(lower, LANES - BLOCK), -lroll(lower, BLOCK))
    both = upper + turned
    g_part[...] = jnp.where(lane < 32, both[0:8], lroll(both[8:16], 32))

    for k in range(1, NTA):
        pltpu.make_async_remote_copy(
            src_ref=g_part, dst_ref=g_ta.at[ta], send_sem=gs1, recv_sem=gr1,
            device_id=(ta_peer(k), ba), device_id_type=MESH,
        ).start()
    g_ta[ta] = g_part[...]
    mine = pl.ds(pl.multiple_of(ba * GROUP, GROUP), GROUP)
    c_full[2 * BLOCK : LANES] = jnp.zeros((LANES - 2 * BLOCK, KEPT), F32)
    cm[...] = c_full[...].T
    corr[0] = cm[mine, 0:BLOCK]
    corr[1] = cm[mine, BLOCK : 2 * BLOCK]
    all_of(g_ta.at[pl.ds(0, NTA - 1)], gr1)
    total = g_ta[0]
    for k in range(1, NTA):
        total = total + g_ta[k]
    g_sum[...] = total
    for k in range(1, NBA):
        pltpu.make_async_remote_copy(
            src_ref=g_sum, dst_ref=g_ba.at[ba], send_sem=gs2, recv_sem=gr2,
            device_id=(ta, ba_peer(k)), device_id_type=MESH,
        ).start()
    g_ba[ba] = g_sum[...]
    all_of(g_ba.at[pl.ds(0, NBA - 1)], gr2)
    total = g_ba[0]
    for k in range(1, NBA):
        total = total + g_ba[k]
    total = total * norm

    gram = jnp.concatenate([total, lroll(total, LANES - 32)], axis=0)
    m_re = jnp.where(lane16 < BLOCK, gram, jnp.where(lane16 == row16 + BLOCK, 1.0, 0.0))
    m_im = jnp.where(lane16 < BLOCK, lroll(gram, LANES - BLOCK), 0.0)
    for c in range(BLOCK):
        scale = lax.rsqrt(m_re[c : c + 1, c : c + 1])
        row_re = m_re[c : c + 1, :] * scale
        row_im = m_im[c : c + 1, :] * scale
        f_re = m_re[:, c : c + 1] * scale
        f_im = m_im[:, c : c + 1] * scale
        below_row = row16 > c
        at_row = row16 == c
        new_re = m_re - (f_re * row_re - f_im * row_im)
        new_im = m_im - (f_re * row_im + f_im * row_re)
        m_re = jnp.where(below_row, new_re, jnp.where(at_row, row_re, m_re))
        m_im = jnp.where(below_row, new_im, jnp.where(at_row, row_im, m_im))

    vm[0:BLOCK] = jnp.where(lane16 < BLOCK, lroll(m_re, LANES - BLOCK), m_im)
    vm[BLOCK : 2 * BLOCK] = jnp.where(lane16 < BLOCK, -lroll(m_im, LANES - BLOCK), m_re)
    v_hi, v_lo = split(vm[:, 0 : 2 * BLOCK])
    v_both = jnp.concatenate([v_hi, v_lo], axis=0)
    for start in range(0, WIDE, step):
        columns = slice(start, start + step)
        both = matmul(v_both, r_hi[:, columns], NN_DIMS)
        low = matmul(v_hi, r_lo[:, columns], NN_DIMS)
        ortho = both[0 : 2 * BLOCK] + both[2 * BLOCK : 4 * BLOCK] + low
        for offset in range(0, step, LANES):
            plane = (start + offset) // LANES
            for ri in range(2):
                part = ortho[ri * BLOCK : (ri + 1) * BLOCK, offset : offset + LANES]
                osend[pl.ds(ri * PLANES + plane, BLOCK, stride=COMPS), :] = part

    for k in range(1, NBA):
        pltpu.make_async_remote_copy(
            src_ref=block_of(osend, ba_peer(k), MINE * COMPS), dst_ref=out.at[:, ba],
            send_sem=os_, recv_sem=or_.at[ba],
            device_id=(ta, ba_peer(k)), device_id_type=MESH,
        ).start()
    pltpu.make_async_copy(block_of(osend, ba, MINE * COMPS), out.at[:, ba], or_.at[ba]).start()
    for copy in (*first_halo, *second_halo, *applied_sends):
        copy.wait_send()
    all_of(basis_all.at[pl.ds(0, (NBA - 1) * GROUP * COMPS)], bs)
    all_of(c_ta.at[pl.ds(0, NTA - 1), pl.ds(0, EARLY)], cs.at[0])
    all_of(c_ta.at[pl.ds(0, NTA - 1), pl.ds(EARLY, NBA // 2 - EARLY)], cs.at[1])
    all_of(c_ba.at[pl.ds(0, NBA - 1)], cs.at[2])
    all_of(g_ta.at[pl.ds(0, NTA - 1)], gs1)
    all_of(g_ba.at[pl.ds(0, NBA - 1)], gs2)
    all_of(osend.at[pl.ds(0, (NBA - 1) * MINE * COMPS)], os_)
    for k in range(NBA):
        place = block_of(osend, ba_peer(k), MINE * COMPS)
        pltpu.make_async_copy(place, out.at[:, ba_peer(k)], or_.at[ba_peer(k)]).wait()


def hand_over(ortho_in, corr_in, ortho_out, corr_out):
    ortho_out[...] = ortho_in[...]
    corr_out[...] = corr_in[...]


def tiles(array):
    times, sites = array.shape[-2:]
    split_up = array.reshape(*array.shape[:-1], sites // LANES, LANES)
    return jnp.swapaxes(split_up, -3, -2).reshape(-1, times * (sites // LANES), LANES)


def untiles(array, shape):
    *lead, times, sites = shape
    split_up = array.reshape(*lead, sites // LANES, times, LANES)
    return jnp.swapaxes(split_up, -3, -2).reshape(shape)


def per_device(search_block, kept_basis, gauge_links, clover_term):
    anywhere = pl.BlockSpec(memory_space=pl.ANY)
    in_vmem = pl.BlockSpec(memory_space=pltpu.VMEM)
    dma = pltpu.SemaphoreType.DMA
    vmem = pltpu.VMEM
    two = 2 * BLOCK
    scratch = [
        vmem((3, MINE * COMPS, 8, LANES), F32),
        vmem((72, 8, LANES), F32),
        vmem((144, 8, LANES), F32),
        vmem((MINE * COMPS, 8, LANES), F32),
        vmem((MINE * 12, 8, LANES), F32),
        vmem((MINE * 12, 8, LANES), F32),
        vmem((2, 12, 8, LANES), F32),
        vmem((2, 12, 8, LANES), F32),
        vmem((2, 12, 8, LANES), F32),
        vmem((2, 12, 8, LANES), F32),
        vmem((KEPT * COMPS, LANES), F32),
        vmem((2 * KEPT, WIDE), BF16),
        vmem((2 * KEPT, WIDE), BF16),
        vmem((BLOCK * COMPS, LANES), F32),
        vmem((two, WIDE), F32),
        vmem((two, 2 * WIDE), BF16),
        vmem((two, 2 * WIDE), BF16),
        vmem((KEPT, LANES), F32),
        vmem((NBA // 2, 8, LANES), F32),
        vmem((two, KEPT), F32),
        vmem((NBA, two, KEPT), F32),
        vmem((NTA, NBA // 2, 8, LANES), F32),
        vmem((LANES, KEPT), F32),
        vmem((2 * two, 2 * KEPT), BF16),
        vmem((two, WIDE), BF16),
        vmem((two, WIDE), BF16),
        vmem((8, LANES), F32),
        vmem((NTA, 8, LANES), F32),
        vmem((8, LANES), F32),
        vmem((NBA, 8, LANES), F32),
        vmem((two, LANES), F32),
        vmem((BLOCK * COMPS, LANES), F32),
        dma((3,)), dma((2, 2)), dma((2, 2)),
        dma, dma((NBA,)), dma((NBA,)), dma((NBA,)), dma((3,)), dma((3,)),
        dma, dma, dma, dma, dma, dma((NBA,)),
    ]
    ortho, correlations = pl.pallas_call(
        kernel,
        out_shape=(
            jax.ShapeDtypeStruct((MINE * COMPS, 8, LANES), F32),
            jax.ShapeDtypeStruct((2, GROUP, BLOCK), F32),
        ),
        in_specs=[anywhere] * 4,
        out_specs=(in_vmem, in_vmem),
        scratch_shapes=scratch,
        compiler_params=pltpu.CompilerParams(
            collective_id=0, has_side_effects=True, vmem_limit_bytes=56 * 1024 * 1024
        ),
    )(tiles(search_block), tiles(kept_basis), tiles(gauge_links), tiles(clover_term))
    ortho, correlations = pl.pallas_call(
        hand_over,
        out_shape=(
            jax.ShapeDtypeStruct(ortho.shape, F32),
            jax.ShapeDtypeStruct(correlations.shape, F32),
        ),
        in_specs=[in_vmem] * 2,
        out_specs=(in_vmem, in_vmem),
    )(ortho, correlations)
    slab = search_block.shape[-2:]
    return untiles(ortho, (MINE, 2, 4, 3, *slab)), correlations


def solution(mesh):
    over_time = P(None, None, None, None, "ta", None)
    grouped = P("ba", None, None, None, "ta", None)
    return jax.shard_map(
        per_device,
        mesh=mesh,
        in_specs=(over_time, grouped, over_time, over_time),
        out_specs=(grouped, P(None, "ba", None)),
        check_vma=False,
    )
```
